32 devices in a mesh: dp: 8 (over z, x), head: 4 (over y, core).
Axes of the slice: x: 2, y: 2, z: 4, core: 2. Of those that a mesh axis runs over, the one named last changes fastest.
Arguments:
- layer_input: bfloat16 [64, 197, 768], P(('dp', 'head')), may hold values from -6 to 6
- prompts: bfloat16 [100, 768], replicated, may hold values from -6 to 6
- lengths: int32 [64], P('dp'), may hold values from 1 to 100, as said below
- key_mask: int32 [64, 297], P('dp'), may hold values 0 or 1
- ln1_gain: float32 [768], replicated, may hold values from 0.1 to 1.9
- ln1_shift: float32 [768], replicated, may hold values from -1.5 to 1.5
- w_qkv: bfloat16 [3, 768, 768], P(None, 'dp', 'head'), may hold values from -0.3125 to 0.3125
- w_out: bfloat16 [768, 768], P('head', 'dp'), may hold values from -0.875 to 0.875
- b_out: float32 [768], replicated, may hold values from -1.5 to 1.5
- ln2_gain: float32 [768], replicated, may hold values from 0.1 to 1.9
- ln2_shift: float32 [768], replicated, may hold values from -1.5 to 1.5
- w_fc1: bfloat16 [768, 3072], P('dp', 'head'), may hold values from -0.21875 to 0.21875
- b_fc1: float32 [3072], P('head'), may hold values from -2.5 to 2.5
- w_fc2: bfloat16 [3072, 768], P('head', 'dp'), may hold values from -0.15625 to 0.15625
- b_fc2: float32 [768], replicated, may hold values from -1.5 to 1.5
- grad_output: bfloat16 [64, 297, 768], P(('dp', 'head')), may hold values from -6 to 6
Outputs:
- layer_output: bfloat16 [64, 297, 768], P(('dp', 'head'))
- grad_input: bfloat16 [64, 197, 768], P(('dp', 'head'))
- grad_prompts: float32 [100, 768], replicated
The draws below stay inside these ranges and needn't reach their ends.
Inputs may be any that keep to these rules, and one draw needn't show every extreme that they name: `lengths`: each length is one of 1, 10, 50 and 100; both 1 and 100 occur.
All inputs are finite; a program needn't handle non-finite values. No bound on the sum of `key_mask` on one device may be relied on, other than what follows from the above.
Results may differ from the reference program's by a relative error of at most 0.019.
Values may be sent and summed in bfloat16 or wider, within the bound.
No kernel may reach another device: no remote copies, remote signals or barrier semaphores. Data moves between devices by JAX's collectives and lax.ppermute only.
A program may use at most 128 MiB of HBM per device.

```python
import jax
import jax.numpy as jnp
from jax import lax

D = 768
HEADS = 12
HEAD_DIM = 64
FF = 3072
IMG_TOK = 197
PROMPTS = 100
SEQ = 297
IMG_DEV = 8
IMAGES = 64


def draw_lengths(key, part):
    table = jnp.array([1, max(1, PROMPTS // 10), PROMPTS // 2, PROMPTS], dtype=jnp.int32)
    picks = jax.random.randint(key, (IMAGES,), 0, 4)
    drawn = table[picks]
    return drawn.at[0].set(PROMPTS).at[1].set(1)


def place_ends(result, stream_key, least, high):
    shape = result.shape
    place = [jax.random.randint(jax.random.fold_in(stream_key, axis), (), 0, shape[axis]) for axis in range(len(shape))]
    result = result.at[tuple(place)].set(least)
    longest = shape.index(max(shape))
    place[longest] = (place[longest] + 1) % shape[longest]
    return result.at[tuple(place)].set(high)


def shard_levels(stream_key, shape, cuts, least, top_value):
    loudness, own = 1.0, jax.random.fold_in(stream_key, 6)
    for axis_at, shards_of in cuts:
        draws = jnp.exp(jax.random.uniform(jax.random.fold_in(own, axis_at), (shards_of,), jnp.float32, least / len(cuts), top_value / len(cuts)))
        loudness = loudness * jnp.repeat(draws, shape[axis_at] // shards_of).reshape([-1 if axis == axis_at else 1 for axis in range(len(shape))])
    return loudness


def scatter_about(own_key, extent, deviation, most, cuts=(), kind=jnp.bfloat16):
    factor_of = shard_levels(own_key, extent, cuts, -0.22, 0.18) if cuts else 1.0
    result = jax.random.normal(own_key, extent, jnp.float32) * deviation * factor_of
    return jnp.minimum(jnp.maximum(result, -most), most).astype(kind)


def setup_inputs(seed: int = 0) -> dict:
    keys = jax.random.split(jax.random.key(seed), 17)
    return {
        "layer_input": scatter_about(keys[0], (IMAGES, IMG_TOK, D), 1.0, 6.0, ((0, 32),)),
        "prompts": scatter_about(keys[1], (PROMPTS, D), 1.0, 6.0),
        "lengths": draw_lengths(jax.random.fold_in(keys[16], 71), 0),
        "key_mask": place_ends((jax.random.randint(keys[3], (IMAGES, SEQ), 0, 8) < 7).astype(jnp.int32), jax.random.fold_in(keys[3], 1), 0, 1),
        "ln1_gain": jnp.clip(1.0 + 0.18 * jax.random.normal(keys[4], (D,), jnp.float32), 0.1, 1.9),
        "ln1_shift": scatter_about(keys[5], (D,), 0.3, 1.5, (), jnp.float32),
        "w_qkv": scatter_about(keys[6], (3, D, D), (D // 2) ** -0.5, 0.3125, ((1, 8), (2, 4))),
        "w_out": scatter_about(keys[7], (D, D), (D // 16) ** -0.5, 0.875, ((0, 4), (1, 8))),
        "b_out": scatter_about(keys[8], (D,), 0.3, 1.5, (), jnp.float32),
        "ln2_gain": jnp.clip(1.0 + 0.18 * jax.random.normal(keys[9], (D,), jnp.float32), 0.1, 1.9),
        "ln2_shift": scatter_about(keys[10], (D,), 0.3, 1.5, (), jnp.float32),
        "w_fc1": scatter_about(keys[11], (D, FF), D ** -0.5, 0.21875, ((0, 8), (1, 4))),
        "b_fc1": scatter_about(keys[12], (FF,), 0.5, 2.5, ((0, 4),), jnp.float32),
        "w_fc2": scatter_about(keys[13], (FF, D), (FF // 2) ** -0.5, 0.15625, ((0, 4), (1, 8))),
        "b_fc2": scatter_about(keys[14], (D,), 0.3, 1.5, (), jnp.float32),
        "grad_output": scatter_about(keys[15], (IMAGES, SEQ, D), 1.0, 6.0, ((0, 32),)),
    }


EPSILON = 1e-06
HIGHEST = lax.Precision.HIGHEST

@jax.custom_vjp
def low(v):
    return lax.optimization_barrier(v.astype(jnp.bfloat16)).astype(jnp.float32)

@jax.custom_vjp
def low_back(v):
    return v

def low_keep(v):
    return (low(v), None)

def low_pass(kept, grad):
    return (grad,)

def back_keep(v):
    return (v, None)

def back_low(kept, grad):
    return (low(grad),)
low.defvjp(low_keep, low_pass)
low_back.defvjp(back_keep, back_low)

def layer_norm(rows, gain, shift):
    center = rows - lax.optimization_barrier(jnp.mean(rows, axis=-1, keepdims=True))
    return center * lax.rsqrt(lax.optimization_barrier(jnp.mean(center * center, axis=-1, keepdims=True)) + EPSILON) * gain + shift

def token_masks(lengths, key_mask):
    position = lax.broadcasted_iota(jnp.int32, key_mask.shape, 1)
    used = (position < IMG_TOK) | (position - IMG_TOK < lengths[:, None])
    seen = (key_mask == 1) | (position == 0)
    return (used, used & seen)

def layer(patches, prompt_rows, used, visible, params):
    gain_one, shift_one, w_qkv, w_out, b_out, gain_two, shift_two, w_fc1, b_fc1, w_fc2, b_fc2 = params
    img_count = patches.shape[0]
    stream = jnp.concatenate([patches, jnp.broadcast_to(prompt_rows[None], (img_count, PROMPTS, D))], axis=1)
    normed = low(layer_norm(stream, gain_one, shift_one))
    projected = low(low_back(jnp.einsum('isd,tdc->tisc', normed, w_qkv, precision=HIGHEST)))
    projected = projected.reshape(3, img_count, SEQ, HEADS, HEAD_DIM)
    scores = low_back(jnp.einsum('ishc,ithc->ihst', projected[0], projected[1], precision=HIGHEST) * HEAD_DIM ** (-0.5))
    scores = jnp.where(visible[:, None, None, :], scores, -1000000000.0)
    attn_probs = low(jax.nn.softmax(scores, axis=-1))
    context = jnp.einsum('ihst,ithc->ishc', attn_probs, projected[2], precision=HIGHEST).reshape(img_count, SEQ, D)
    context = low(low_back(context))
    attn_out = low_back(jnp.einsum('isc,cd->isd', context, w_out, precision=HIGHEST))
    hidden_mid = stream + attn_out + b_out
    normed_two = low(layer_norm(hidden_mid, gain_two, shift_two))
    pre_act = low_back(jnp.einsum('isd,df->isf', normed_two, w_fc1, precision=HIGHEST) + b_fc1)
    active = low(low_back(jax.nn.gelu(pre_act, approximate=False)))
    mlp_out = low_back(jnp.einsum('isf,fd->isd', active, w_fc2, precision=HIGHEST))
    return (hidden_mid + mlp_out + b_fc2) * used[..., None].astype(jnp.float32)

def reference(layer_input, prompts, lengths, key_mask, ln1_gain, ln1_shift, w_qkv, w_out, b_out, ln2_gain, ln2_shift, w_fc1, b_fc1, w_fc2, b_fc2, grad_output):
    params = tuple((weight_arr.astype(jnp.float32) for weight_arr in (ln1_gain, ln1_shift, w_qkv, w_out, b_out, ln2_gain, ln2_shift, w_fc1, b_fc1, w_fc2, b_fc2)))
    used, visible = token_masks(lengths, key_mask)
    groups = IMAGES // IMG_DEV

    def regroup(array_in):
        return array_in.reshape((groups, IMG_DEV) + array_in.shape[1:])
    prompt_rows = prompts.astype(jnp.float32)

    def step(running, pieces):
        patches, used_rows, visible_rows, cotangent = pieces

        def forward(patch_rows, prompt_part):
            return layer(patch_rows, prompt_part, used_rows, visible_rows, params)
        output, backward = jax.vjp(forward, patches.astype(jnp.float32), prompt_rows)
        grad_patch, grad_prompt = backward(cotangent.astype(jnp.float32))
        return (running + grad_prompt, (output.astype(jnp.bfloat16), grad_patch.astype(jnp.bfloat16)))
    running, (outputs, grad_patches) = lax.scan(step, jnp.zeros((PROMPTS, D), jnp.float32), (regroup(layer_input), regroup(used), regroup(visible), regroup(grad_output)))
    return (outputs.reshape(IMAGES, SEQ, D), grad_patches.reshape(IMAGES, IMG_TOK, D), running)
```

```python
import functools

import jax
import jax.numpy as jnp
from jax import lax
from jax.experimental import pallas as pl
from jax.experimental.pallas import tpu as pltpu
from jax.sharding import PartitionSpec as P

HEAD_DIM = 64
IMG_TOK = 197
PROMPTS = 100
SEQ = IMG_TOK + PROMPTS
ROWS = 304
KEYS = 384
EPSILON = 1e-06
BOTH = ("dp", "head")
F32 = jnp.float32
BF16 = jnp.bfloat16

NN = (((1,), (0,)), ((), ()))
NT = (((1,), (1,)), ((), ()))
TN = (((0,), (0,)), ((), ()))


def dot(left, right, dims):
    return lax.dot_general(left, right, dims, preferred_element_type=F32)


def device_perm(count, target):
    pairs = []
    for index in range(count):
        c, y, x, z = index % 2, index // 2 % 2, index // 4 % 2, index // 8
        z, x, y, c = target(z, x, y, c)
        pairs.append((index, ((z * 2 + x) * 2 + y) * 2 + c))
    return pairs


class Exchange:
    def __init__(self, dp, head):
        self.count = dp * head
        self.depth = dp // 2

    def move(self, value, target):
        return lax.ppermute(value, BOTH, device_perm(self.count, target))

    def from_z(self, value, step):
        depth = self.depth
        return self.move(value, lambda z, x, y, c: ((z - step) % depth, x, y, c))

    def first(self, value):
        return self.move(value, lambda z, x, y, c: (z, x ^ (1 - c), y ^ c, c))

    def second(self, value):
        return self.move(value, lambda z, x, y, c: (z, x ^ c, y ^ (1 - c), c))

    def core(self, value):
        return self.move(value, lambda z, x, y, c: (z, x, y, 1 - c))

    def swap(self, value, dz=0, dx=0, dy=0):
        return self.move(value, lambda z, x, y, c: (z ^ dz, x ^ dx, y ^ dy, c))


def gather_pieces(exchange, piece, groups):
    arrived = {0: piece}
    for step in (1, 3, 2):
        arrived[step] = exchange.from_z(piece, step)
    arrays, plan = [], []
    for group in groups:
        base = jnp.stack([arrived[step] for step in group])
        near = jnp.concatenate([base, exchange.first(base)])
        far = exchange.second(near)
        for is_other, held in ((0, (near, far)), (1, (exchange.core(near), exchange.core(far)))):
            for is_far, array in enumerate(held):
                arrays.append(array)
                plan.append([(step, half, is_far, is_other) for half in (0, 1) for step in group])
    return arrays, plan


def placement(entry, place, depth):
    z, x, y, c = place
    step, half, is_far, is_other = entry
    core = c if not is_other else 1 - c
    moved_first, moved_second = half, is_far
    dx = jnp.where(core == 0, moved_first, moved_second)
    dy = jnp.where(core == 0, moved_second, moved_first)
    row = lax.rem(z + step, depth) * 2 + jnp.where(dx == 1, 1 - x, x)
    return dy * 2 + is_other, row


def load_weights(pieces, plan, place_ref, store, sems, depth):
    if plan is None:
        for slot in range(store.shape[0]):
            pltpu.make_async_copy(pieces[0].at[slot], store.at[slot], sems.at[slot]).start()
        return
    place = tuple(place_ref[i] for i in range(4))
    for ref, entries in zip(pieces, plan):
        for index, entry in enumerate(entries):
            slot, block = placement(entry, place, depth)
            rows = ref.shape[1]
            start = pl.multiple_of(block * rows, rows)
            pltpu.make_async_copy(
                ref.at[index], store.at[slot, pl.ds(start, rows)], sems.at[slot]
            ).start()


def wait_slot(store, sems, slot):
    pltpu.make_async_copy(store.at[slot], store.at[slot], sems.at[slot]).wait()


def row_mean(value):
    return jnp.mean(value, axis=-1, keepdims=True)


def normalized(rows):
    center = rows - row_mean(rows)
    scale = lax.rsqrt(row_mean(center * center) + EPSILON)
    return center * scale, scale


def norm_back(grad, gain, unit, scale):
    grad = grad * gain
    return scale * (grad - row_mean(grad) - unit * row_mean(grad * unit))


def low_lanes(shape):
    return lax.broadcasted_iota(jnp.int32, shape, len(shape) - 1) < HEAD_DIM


def half_of(tile, keep_low):
    keep = low_lanes(tile.shape)
    zero = jnp.zeros_like(tile)
    return jnp.where(keep, tile, zero) if keep_low else jnp.where(keep, zero, tile)


def attend_kernel(plan, depth, images, *refs):
    place, normed, stream, visible, b_out, gain, shift = refs[:7]
    count = 1 if plan is None else len(plan)
    pieces = refs[7 : 7 + count]
    qkv_out, probs_out, mid_out, normed_out, store, total, sems = refs[7 + count :]
    slot = pl.program_id(0)

    @pl.when(slot == 0)
    def _():
        load_weights(pieces, plan, place, store, sems, depth)
        total[...] = jnp.zeros_like(total)

    wait_slot(store, sems, slot)
    qkv = dot(normed[...], store[slot, :, :640], NN)
    for image in range(images):
        rows = slice(image * ROWS, (image + 1) * ROWS)
        qkv_out[0, image, :ROWS] = qkv[rows].astype(BF16)
        qkv_out[0, image, ROWS:] = jnp.zeros((KEYS - ROWS, 640), BF16)
    for image in range(images):
        rows = slice(image * ROWS, (image + 1) * ROWS)
        see = visible[image] > 0
        mixed = []
        for head in range(3):
            low = head != 1
            query_at, key_at, value_at = (0, 128, 256) if head < 2 else (384, 512, 384)
            query = half_of(qkv_out[0, image, :ROWS, query_at : query_at + 128], low)
            query = query * jnp.asarray(0.125, BF16)
            keys = qkv_out[0, image, :, key_at : key_at + 128]
            values = half_of(qkv_out[0, image, :, value_at : value_at + 128], head == 0)
            scores = jnp.where(see, dot(query, keys, NT), -1000000000.0)
            weight = jnp.exp(scores - jnp.max(scores, axis=-1, keepdims=True))
            probs = weight * (1.0 / jnp.sum(weight, axis=-1, keepdims=True))
            probs_b = probs.astype(BF16)
            probs_out[0, image * 3 + head] = probs_b
            mixed.append(dot(probs_b, values, NN))
        context = jnp.concatenate([mixed[2], mixed[0] + mixed[1]], axis=1).astype(BF16)
        total[rows] += dot(context, store[slot, :, 512:], NT)

    @pl.when(slot == pl.num_programs(0) - 1)
    def _():
        mid = stream[...].astype(F32) + total[...] + b_out[...]
        mid_out[...] = mid
        normed_out[...] = (normalized(mid)[0] * gain[...] + shift[...]).astype(BF16)


def gelu_parts(pre):
    density = jnp.exp(pre * pre * -0.5) * 0.3989422804014327
    chance = 0.5 + 0.5 * lax.erf(pre * 0.7071067811865476)
    return chance, density


def mlp_kernel(plan, depth, width, first, *refs):
    place, normed, grad, bias = refs[:4]
    refs = refs[4:]
    if not first:
        out_in, back_in = refs[:2]
        refs = refs[2:]
    count = 1 if plan is None else len(plan)
    pieces = refs[:count]
    out_sum, back_sum, store, sems = refs[count:]
    slot = pl.program_id(0)

    @pl.when(slot == 0)
    def _():
        load_weights(pieces, plan, place, store, sems, depth)
        if first:
            out_sum[...] = jnp.zeros_like(out_sum)
            back_sum[...] = jnp.zeros_like(back_sum)
        else:
            out_sum[...] = out_in[...]
            back_sum[...] = back_in[...]

    wait_slot(store, sems, slot)
    half = normed.shape[0] // 2
    for part in range(2):
        rows = slice(part * half, (part + 1) * half)
        pre = dot(normed[rows], store[slot, :, :width], NN) + bias[0]
        chance, density = gelu_parts(pre)
        active = (pre * chance).astype(BF16)
        slope = chance + pre * density
        out_sum[rows] += dot(active, store[slot, :, width:], NT)
        grad_active = dot(grad[rows], store[slot, :, width:], NN).astype(BF16).astype(F32)
        grad_pre = (grad_active * slope).astype(BF16)
        back_sum[rows] += dot(grad_pre, store[slot, :, :width], NT)


def back_kernel(plan, depth, images, *refs):
    place, lengths, mid, mlp_out, grad_normed, grad, stream, qkv, probs = refs[:9]
    gain_two, b_fc2, gain_one = refs[9:12]
    count = 1 if plan is None else len(plan)
    pieces = refs[12 : 12 + count]
    result, grad_input, grad_prompts, store, total, grad_mid, grad_attn, stacked, sems = refs[12 + count :]
    slot = pl.program_id(0)

    @pl.when(slot == 0)
    def _():
        load_weights(pieces, plan, place, store, sems, depth)
        total[...] = jnp.zeros_like(total)
        position = lax.broadcasted_iota(jnp.int32, (ROWS, 1), 0)
        for image in range(images):
            rows = slice(image * ROWS, (image + 1) * ROWS)
            used = (position < IMG_TOK + lengths[image]).astype(F32)
            rows_out = (mid[rows] + mlp_out[rows] + b_fc2[...]) * used
            result[image] = rows_out[:SEQ].astype(BF16)
            unit, scale = normalized(mid[rows])
            back = grad[rows].astype(F32) + norm_back(grad_normed[rows], gain_two[...], unit, scale)
            grad_mid[rows] = back
            grad_attn[rows] = back.astype(BF16)

    wait_slot(store, sems, slot)
    grad_context = dot(grad_attn[...], store[slot, :, 512:], NN).astype(BF16)
    for image in range(images):
        rows = slice(image * ROWS, (image + 1) * ROWS)
        tiles = {}

        def add(at, value):
            tiles[at] = value if at not in tiles else tiles[at] + value

        for head in range(3):
            low = head == 0
            grad_at = 128 if head < 2 else 0
            query_at, key_at, value_at = (0, 128, 256) if head < 2 else (384, 512, 384)
            grad_mix = half_of(grad_context[rows, grad_at : grad_at + 128], low)
            query = half_of(qkv[0, image, :ROWS, query_at : query_at + 128], head != 1)
            query = query * jnp.asarray(0.125, BF16)
            keys = half_of(qkv[0, image, :, key_at : key_at + 128], head != 1)
            keys = keys * jnp.asarray(0.125, BF16)
            values = qkv[0, image, :, value_at : value_at + 128]
            probs_b = probs[0, image * 3 + head]
            weight = probs_b.astype(F32)
            grad_probs = dot(grad_mix, values, NT)
            grad_scores = weight * (
                grad_probs - jnp.sum(weight * grad_probs, axis=-1, keepdims=True)
            )
            grad_scores = grad_scores.astype(BF16)
            add(value_at, dot(probs_b, grad_mix, TN)[:ROWS])
            add(query_at, dot(grad_scores, keys, NN))
            add(key_at, dot(grad_scores, query, TN)[:ROWS])
        for at, value in tiles.items():
            stacked[rows, at : at + 128] = value.astype(BF16)
    total[...] += dot(stacked[...], store[slot, :, :640], NT)

    @pl.when(slot == pl.num_programs(0) - 1)
    def _():
        prompt_sum = None
        for image in range(images):
            rows = slice(image * ROWS, (image + 1) * ROWS)
            unit, scale = normalized(stream[rows].astype(F32))
            back = grad_mid[rows] + norm_back(total[rows], gain_one[...], unit, scale)
            grad_input[image] = back[:IMG_TOK].astype(BF16)
            part = back[IMG_TOK:SEQ]
            prompt_sum = part if prompt_sum is None else prompt_sum + part
        grad_prompts[...] = prompt_sum


def whole(shape):
    return pl.BlockSpec(shape, lambda s: (0,) * len(shape))


ANY = pl.BlockSpec(memory_space=pl.ANY)
SMEM = pl.BlockSpec(memory_space=pltpu.SMEM)


def cost(flops, nbytes):
    return pl.CostEstimate(flops=int(flops), bytes_accessed=int(nbytes), transcendentals=0)


def attend(plan, depth, images, place, normed, stream, visible, b_out, gain, shift, pieces):
    rows, width = normed.shape
    slots = 4
    return pl.pallas_call(
        functools.partial(attend_kernel, plan, depth, images),
        grid=(slots,),
        in_specs=[
            SMEM,
            whole((rows, width)),
            whole((rows, width)),
            whole((images, 1, KEYS)),
            whole((1, width)),
            whole((1, width)),
            whole((1, width)),
        ]
        + [ANY] * len(pieces),
        out_specs=[
            pl.BlockSpec((1, images, KEYS, 640), lambda s: (s, 0, 0, 0)),
            pl.BlockSpec((1, images * 3, ROWS, KEYS), lambda s: (s, 0, 0, 0)),
            whole((rows, width)),
            whole((rows, width)),
        ],
        out_shape=[
            jax.ShapeDtypeStruct((slots, images, KEYS, 640), BF16),
            jax.ShapeDtypeStruct((slots, images * 3, ROWS, KEYS), BF16),
            jax.ShapeDtypeStruct((rows, width), F32),
            jax.ShapeDtypeStruct((rows, width), BF16),
        ],
        scratch_shapes=[
            pltpu.VMEM((slots, width, 768), BF16),
            pltpu.VMEM((rows, width), F32),
            pltpu.SemaphoreType.DMA((slots,)),
        ],
        compiler_params=pltpu.CompilerParams(vmem_limit_bytes=50 << 20),
        cost_estimate=cost(6e9, 1.6e7),
    )(place, normed, stream, visible, b_out, gain, shift, *pieces)


def mlp(plan, depth, place, normed, grad, bias, sums, pieces):
    rows, width = normed.shape
    slots, chunk = bias.shape[0], bias.shape[2]
    first = sums is None
    sums = () if first else tuple(sums)
    return pl.pallas_call(
        functools.partial(mlp_kernel, plan, depth, chunk, first),
        grid=(slots,),
        in_specs=[SMEM, whole((rows, width)), whole((rows, width))]
        + [pl.BlockSpec((1, 1, chunk), lambda s: (s, 0, 0))]
        + [whole((rows, width))] * len(sums)
        + [ANY] * len(pieces),
        out_specs=[whole((rows, width))] * 2,
        out_shape=[jax.ShapeDtypeStruct((rows, width), F32)] * 2,
        scratch_shapes=[
            pltpu.VMEM((slots, width, 2 * chunk), BF16),
            pltpu.SemaphoreType.DMA((slots,)),
        ],
        compiler_params=pltpu.CompilerParams(vmem_limit_bytes=50 << 20),
        cost_estimate=cost(8.0 * rows * width * chunk * slots, 1.6e7),
    )(place, normed, grad, bias, *sums, *pieces)


def attend_back(
    plan, depth, images, place, lengths, mid, mlp_out, grad_normed, grad, stream, qkv, probs,
    gain_two, b_fc2, gain_one, pieces,
):
    rows, width = mid.shape
    slots = 4
    row = whole((1, width))
    full = whole((rows, width))
    return pl.pallas_call(
        functools.partial(back_kernel, plan, depth, images),
        grid=(slots,),
        in_specs=[SMEM, SMEM, full, full, full, full, full]
        + [
            pl.BlockSpec((1, images, KEYS, 640), lambda s: (s, 0, 0, 0)),
            pl.BlockSpec((1, images * 3, ROWS, KEYS), lambda s: (s, 0, 0, 0)),
        ]
        + [row] * 3
        + [ANY] * len(pieces),
        out_specs=[
            whole((images, SEQ, width)),
            whole((images, IMG_TOK, width)),
            whole((PROMPTS, width)),
        ],
        out_shape=[
            jax.ShapeDtypeStruct((images, SEQ, width), BF16),
            jax.ShapeDtypeStruct((images, IMG_TOK, width), BF16),
            jax.ShapeDtypeStruct((PROMPTS, width), F32),
        ],
        scratch_shapes=[
            pltpu.VMEM((slots, width, 768), BF16),
            pltpu.VMEM((rows, width), F32),
            pltpu.VMEM((rows, width), F32),
            pltpu.VMEM((rows, width), BF16),
            pltpu.VMEM((rows, 640), BF16),
            pltpu.SemaphoreType.DMA((slots,)),
        ],
        compiler_params=pltpu.CompilerParams(vmem_limit_bytes=50 << 20),
        cost_estimate=cost(7e9, 2.4e7),
    )(
        place, lengths, mid, mlp_out, grad_normed, grad, stream, qkv, probs,
        gain_two, b_fc2, gain_one, *pieces,
    )


def layer_norm(rows, gain, shift):
    return normalized(rows)[0] * gain + shift


def sum_prompts(exchange, partial):
    half = partial.shape[1] // 2
    core = lax.axis_index("head") % 2
    low, high = partial[:, :half], partial[:, half:]
    keep = jnp.where(core == 0, low, high)
    give = jnp.where(core == 0, high, low)
    mine = keep + exchange.core(give.astype(BF16)).astype(F32)
    for move in ({"dx": 1}, {"dy": 1}, {"dz": 1}, {"dz": 2}):
        mine = lax.reduce_precision(mine, 8, 7)
        mine = mine + exchange.swap(mine.astype(BF16), **move).astype(F32)
    mine = lax.reduce_precision(mine, 8, 7)
    other = exchange.core(mine.astype(BF16)).astype(F32)
    return jnp.where(
        core == 0,
        jnp.concatenate([mine, other], axis=1),
        jnp.concatenate([other, mine], axis=1),
    )


def per_device(
    exchange,
    layer_input,
    prompts,
    lengths,
    key_mask,
    ln1_gain,
    ln1_shift,
    w_qkv,
    w_out,
    b_out,
    ln2_gain,
    ln2_shift,
    w_fc1,
    b_fc1,
    w_fc2,
    b_fc2,
    grad_output,
):
    images, _, width = layer_input.shape
    chunks = (256, 512)

    out_t, fc2_t = w_out.T, w_fc2.T
    query, key, value = w_qkv[0], w_qkv[1], w_qkv[2]
    piece_attn = jnp.concatenate(
        [query[:, :128], key[:, :128], value[:, :128], query[:, 128:], value[:, 128:]]
        + [key[:, 128:], out_t[:, 128:], out_t[:, :128]],
        axis=1,
    )
    pieces_mlp, start = [], 0
    for chunk in chunks:
        pieces_mlp.append(
            jnp.concatenate(
                [w_fc1[:, start : start + chunk], fc2_t[:, start : start + chunk]], axis=1
            )
        )
        start += chunk

    if exchange is not None:
        depth = exchange.depth
        dp, head = lax.axis_index("dp"), lax.axis_index("head")
        place = jnp.stack([dp // 2, dp % 2, head // 2, head % 2]).astype(jnp.int32)
        attn, plan_attn = gather_pieces(exchange, piece_attn, ((0,), (1, 3, 2)))
        gathered = [gather_pieces(exchange, piece, ((0,), (1, 3, 2))) for piece in pieces_mlp]
        bias = jnp.stack([b_fc1, exchange.core(b_fc1)])
        bias = jnp.concatenate([bias, exchange.swap(bias, dy=1)])
    else:
        depth = 0
        place = jnp.zeros((4,), jnp.int32)

        def gather_whole(piece):
            rows = lax.all_gather(piece, "dp", axis=0, tiled=True)
            return [lax.all_gather(rows, "head", axis=0)], None

        attn, plan_attn = gather_whole(piece_attn)
        gathered = [gather_whole(piece) for piece in pieces_mlp]
        bias = lax.all_gather(b_fc1, "head", axis=0)

    own_at = lax.axis_index("head") * images
    own_lengths = lax.dynamic_slice_in_dim(lengths, own_at, images, 0)
    own_mask = lax.dynamic_slice_in_dim(key_mask, own_at, images, 0)
    position = lax.broadcasted_iota(jnp.int32, (images, SEQ), 1)
    used = (position < IMG_TOK) | (position - IMG_TOK < own_lengths[:, None])
    visible = used & ((own_mask == 1) | (position == 0))
    visible = jnp.pad(visible.astype(F32), ((0, 0), (0, KEYS - SEQ)))[:, None, :]
    prompt_rows = jnp.broadcast_to(prompts[None], (images, PROMPTS, width))
    padding = jnp.zeros((images, ROWS - SEQ, width), BF16)
    stream = jnp.concatenate([layer_input, prompt_rows, padding], axis=1)
    stream = stream.reshape(images * ROWS, width)
    grad = jnp.where(used[:, :, None], grad_output, jnp.zeros_like(grad_output))
    grad = jnp.concatenate([grad, padding], axis=1).reshape(images * ROWS, width)
    normed = layer_norm(stream.astype(F32), ln1_gain, ln1_shift).astype(BF16)

    row = lambda vector: vector.reshape(1, width)
    qkv, probs, mid, normed_mlp = attend(
        plan_attn, depth, images, place, normed, stream, visible,
        row(b_out), row(ln2_gain), row(ln2_shift), attn,
    )
    sums, start = None, 0
    for chunk, (pieces, plan) in zip(chunks, gathered):
        chunk_bias = bias[:, None, start : start + chunk]
        sums = mlp(plan, depth, place, normed_mlp, grad, chunk_bias, sums, pieces)
        start += chunk
    result, grad_input, partial = attend_back(
        plan_attn, depth, images, place, own_lengths, mid, sums[0], sums[1], grad, stream,
        qkv, probs, row(ln2_gain), row(b_fc2), row(ln1_gain), attn,
    )
    if exchange is not None:
        grad_prompts = sum_prompts(exchange, partial)
    else:
        grad_prompts = lax.psum(partial, BOTH)
    return (result, grad_input, grad_prompts)


def solution(mesh):
    dp, head = mesh.shape["dp"], mesh.shape["head"]
    exchange = Exchange(dp, head) if (dp, head) == (8, 4) else None
    placed = (
        P(BOTH, None, None),
        P(),
        P("dp"),
        P("dp", None),
        P(),
        P(),
        P(None, "dp", "head"),
        P("head", "dp"),
        P(),
        P(),
        P(),
        P("dp", "head"),
        P("head"),
        P("head", "dp"),
        P(),
        P(BOTH, None, None),
    )
    return jax.shard_map(
        functools.partial(per_device, exchange),
        mesh=mesh,
        in_specs=placed,
        out_specs=(P(BOTH, None, None), P(BOTH, None, None), P()),
        check_vma=False,
    )
```

```python
import functools

import jax
import jax.numpy as jnp
from jax import lax
from jax.experimental import pallas as pl
from jax.experimental.pallas import tpu as pltpu
from jax.sharding import PartitionSpec as P

HEAD_DIM = 64
IMG_TOK = 197
PROMPTS = 100
SEQ = IMG_TOK + PROMPTS
ROWS = 304
KEYS = 384
EPSILON = 1e-06
GRANTS = (9, 9, 9, 11)
COST_SCALE = 10.0
CHUNKS = (256, 256, 256)
BOTH = ("dp", "head")
F32 = jnp.float32
BF16 = jnp.bfloat16

NN = (((1,), (0,)), ((), ()))
NT = (((1,), (1,)), ((), ()))
TN = (((0,), (0,)), ((), ()))


def dot(left, right, dims):
    return lax.dot_general(left, right, dims, preferred_element_type=F32)


def device_perm(count, target):
    pairs = []
    for index in range(count):
        c, y, x, z = index % 2, index // 2 % 2, index // 4 % 2, index // 8
        z, x, y, c = target(z, x, y, c)
        pairs.append((index, ((z * 2 + x) * 2 + y) * 2 + c))
    return pairs


def along_ring(z, step, depth):
    place = ((z ^ (z >> 1)) + step + depth) % depth
    return place ^ (place >> 1)


class Exchange:
    def __init__(self, dp, head):
        self.count = dp * head
        self.depth = dp // 2

    def move(self, value, target):
        return lax.ppermute(value, BOTH, device_perm(self.count, target))

    def from_z(self, value, step):
        return self.move(value, lambda z, x, y, c: (along_ring(z, -step, self.depth), x, y, c))

    def first(self, value):
        return self.move(value, lambda z, x, y, c: (z, x ^ (1 - c), y ^ c, c))

    def second(self, value):
        return self.move(value, lambda z, x, y, c: (z, x ^ c, y ^ (1 - c), c))

    def core(self, value):
        return self.move(value, lambda z, x, y, c: (z, x, y, 1 - c))

    def swap(self, value, dz=0, dx=0, dy=0):
        return self.move(value, lambda z, x, y, c: (z ^ dz, x ^ dx, y ^ dy, c))


def tie(*values):
    return lax.optimization_barrier(values)


ALL, UP, DOWN = range(3)
NEAR_FAR = ((0, 0), (1, 0), (0, 1), (1, 1))


class Held:
    def __init__(self, exchange):
        self.exchange = exchange
        self.arrays, self.plan = [], []

    def add(self, array, lane, steps, halves, is_other=0, kind=ALL):
        self.arrays.append(array)
        entries = [(step, half, is_far, is_other) for half, is_far in halves for step in steps]
        self.plan.append((lane, kind, entries))

    def add_both(self, array, steps, halves):
        self.add(array, 0, steps, halves, 0)
        self.add(self.exchange.core(array), 0, steps, halves, 1)

    def add_pair(self, pair, lane, steps, halves, kind=ALL):
        for is_other, array in enumerate(pair):
            self.add(array, lane, steps, halves, is_other, kind)


class Gather:
    def __init__(self, exchange, own, both, later, bias):
        self.exchange, self.width, self.part = exchange, own.shape[1], later.shape[1] // 2
        own, both, self.later, self.bias = own[None], both[None], later[None], bias
        first = exchange.first(both)
        self.came = jnp.concatenate([exchange.from_z(own, 1), exchange.from_z(own, 3)])
        self.own = both, first

    def attention(self, *ready):
        exchange, width, part = self.exchange, self.width, self.part
        both, first, came, later, bias = tie(*self.own, self.came, self.later, self.bias)
        near = jnp.concatenate([both, first])
        own_far = exchange.second(near)
        two = exchange.from_z(came[:1], 1)
        other = exchange.core(bias)
        at_low = lax.axis_index("head") % 2 == 0
        bias = jnp.where(at_low, jnp.stack([bias, other]), jnp.stack([other, bias]))
        own_near, own_far, base, later, bias, *ready = tie(
            near, own_far, jnp.concatenate([came, two]), later, bias, *ready
        )
        first = exchange.first(base)
        later_one = exchange.from_z(later, 1)
        owns = (own_near, own_far, exchange.core(own_near), exchange.core(own_far))
        near, later_one, later, bias, *owns = tie(
            jnp.concatenate([base, first]), later_one, later, bias, *owns
        )
        far = exchange.second(near)
        later_three = exchange.from_z(later, 3)
        later_two = exchange.from_z(later_one, 1)
        other_near = exchange.core(near)
        self.bias = jnp.concatenate([bias, exchange.swap(bias, dy=1)])
        far, base, self.plane, self.bias = tie(
            far,
            jnp.concatenate([later, later_one, later_three, later_two]),
            jnp.concatenate([owns[0][:, :, width:], owns[1][:, :, width:]]),
            self.bias,
        )
        near_later = jnp.concatenate([base, exchange.first(base)])
        self.up = exchange.from_z(self.plane, 1)
        self.later_near, self.up, self.plane = tie(near_later, self.up, self.plane)
        self.split = part + part // 2
        self.later_far = exchange.second(self.later_near[:, :, : self.split])
        self.other_near = exchange.core(self.later_near)
        self.down = exchange.from_z(self.plane, 3)
        self.low = exchange.from_z(self.up[:2], 1)

        held = Held(exchange)
        self.parts = [Held(exchange) for _ in range(3)]
        for index, array in enumerate(owns):
            halves = NEAR_FAR[2 * (index % 2) : 2 * (index % 2) + 2]
            held.add(array, 0, (0,), halves, index // 2)
            self.parts[1].add(array, width, (0,), halves, index // 2)
        held.add(near, 0, (1, 3, 2), NEAR_FAR[:2], 0)
        held.add(other_near, 0, (1, 3, 2), NEAR_FAR[:2], 1)
        held.add_both(far, (1, 3, 2), NEAR_FAR[2:])
        return held, ready

    def round_seven(self, token):
        exchange, steps = self.exchange, (0, 1, 3, 2)
        near, far, up, down, low, token = tie(
            self.later_near, self.later_far, self.up, self.down, self.low, token
        )
        self.rest = exchange.second(near[:, :, self.split :])
        self.high = exchange.from_z(down[2:], 3)
        near, far = (near, self.other_near), (far, exchange.core(far))
        self.parts[2].add_pair(near, self.part, steps, NEAR_FAR[:2])
        self.parts[2].add_pair(far, self.part, steps, NEAR_FAR[2:], UP)
        self.halves = [Held(exchange), Held(exchange)]
        for is_other, held in enumerate(self.halves):
            held.add(near[is_other], 0, steps, NEAR_FAR[:2], is_other)
            held.add(far[is_other], 0, steps, NEAR_FAR[2:], is_other)
        self.parts[1].add_both(up, (1,), NEAR_FAR)
        self.parts[1].add_both(down, (3,), NEAR_FAR)
        self.parts[1].add_both(low, (2,), NEAR_FAR[:2])
        return token

    def round_eight(self, token):
        high, rest, token = tie(self.high, self.rest, token)
        self.parts[1].add_both(high, (2,), NEAR_FAR[2:])
        self.parts[2].add_pair((rest, self.exchange.core(rest)), 0, (0, 1, 3, 2), NEAR_FAR[2:], DOWN)
        return token


def placement(entry, place, depth):
    z, x, y, c = place
    step, half, is_far, is_other = entry
    core = 1 - c if is_other else c
    dx = jnp.where(core == 0, half, is_far)
    dy = jnp.where(core == 0, is_far, half)
    block = along_ring(z, step, depth) * 2 + jnp.where(dx == 1, 1 - x, x)
    return block, dy, core


def row_mean(value):
    return jnp.mean(value, axis=-1, keepdims=True)


def normalized(rows):
    center = rows - row_mean(rows)
    scale = lax.rsqrt(row_mean(center * center) + EPSILON)
    return center * scale, scale


def norm_back(grad, gain, unit, scale):
    grad = grad * gain
    return scale * (grad - row_mean(grad) - unit * row_mean(grad * unit))


def low_lanes(rows):
    return lax.broadcasted_iota(jnp.int32, (rows, 128), 1) < HEAD_DIM


def both_halves(tile, keep):
    zero = jnp.zeros_like(tile)
    return jnp.concatenate([jnp.where(keep, tile, zero), jnp.where(keep, zero, tile)], axis=0)


def side_to_rows(pair):
    return jnp.concatenate([pair[:, :KEYS], pair[:, KEYS:]], axis=0)


def by_blocks(rows, size, body):
    @pl.loop(0, rows // size)
    def _(index):
        body(pl.ds(pl.multiple_of(index * size, size), size))


class Loader:
    def __init__(self, plan, depth):
        self.plan, self.depth = plan, depth
        self.count = len(plan)

    def run(self, place_ref, pieces, put):
        place = tuple(place_ref[i] for i in range(4))
        for ref, (lane, kind, entries) in zip(pieces, self.plan):
            for index, entry in enumerate(entries):
                rows = ref.shape[1]
                if self.depth:
                    block, dy, core = placement(entry, place, self.depth)
                    where = pl.ds(pl.multiple_of(block * rows, rows), rows)
                else:
                    (dy, core), where = entry, pl.ds(0, rows)
                put(ref.at[index, :, lane:], where, dy, core, kind)


def lanes_at(start, size):
    return pl.ds(pl.multiple_of(start, 128), size)


def put_attn(wide, out, raw):
    def put(source, rows, dy, core, kind):
        slot = dy * 2 + core
        wide[dy, rows, lanes_at(core * 384, 384)] = source[:, :384]
        out[rows, lanes_at(slot * 128, 128)] = source[:, 384:512]
        raw[rows, lanes_at(slot * 256, 256)] = source[:, 512:768]

    return put


def join_thirds(raw, dy, wide, out):
    even, odd = raw[:, dy * 512 : dy * 512 + 256], raw[:, dy * 512 + 256 : dy * 512 + 512]
    low = low_lanes(even.shape[0])
    at = dy * 384
    wide[:, at : at + 128] = jnp.where(low, even[:, :128], odd[:, :128])
    wide[:, at + 128 : at + 256] = jnp.where(low, even[:, 128:], odd[:, 128:])
    wide[:, at + 256 : at + 384] = jnp.where(low, odd[:, :128], even[:, :128])
    out[:, dy * 128 : dy * 128 + 128] = jnp.where(low, odd[:, 128:], even[:, 128:])


def put_mlp(up, down, chunk, slots):
    def put(source, rows, dy, core, kind):
        lanes = lanes_at((dy if slots == 2 else dy * 2 + core) * chunk, chunk)
        if kind != DOWN:
            up[rows, lanes] = source[:, :chunk]
        if kind != UP:
            start = 0 if kind == DOWN else chunk
            down[rows, lanes] = source[:, start : start + chunk]

    return put


def attend_units(images, pair, normed, weights, visible, qkv_out, exps_out, ctx_out, inv_out):
    qkv = dot(normed[...], weights, NN)
    low = low_lanes(KEYS)
    keep = jnp.logical_xor(low, pair == 2)
    counts = both_halves(jnp.ones((KEYS, 128), BF16), keep)
    padding = jnp.zeros((KEYS - ROWS, 128), BF16)
    for image in range(images):
        rows = slice(image * ROWS, (image + 1) * ROWS)
        see = visible[image] > 0
        for unit in range(2):
            tiles = [qkv[rows, unit * 384 + at : unit * 384 + at + 128] for at in (0, 128, 256)]
            query = (tiles[0] * 0.125).astype(BF16)
            key, value = (
                jnp.concatenate([tile.astype(BF16), padding], axis=0) for tile in tiles[1:]
            )
            qkv_out[pair, unit, image, :ROWS, :128] = query
            qkv_out[pair, unit, image, :, 128:256] = key
            qkv_out[pair, unit, image, :, 256:] = value
            scores = dot(query, both_halves(key, low), NT)
            parts = []
            for head in range(2):
                part = jnp.where(see, scores[:, head * KEYS : (head + 1) * KEYS], -1000000000.0)
                part = jnp.exp(part - jnp.max(part, axis=-1, keepdims=True))
                parts.append(part.astype(BF16))
            exps = jnp.concatenate(parts, axis=1)
            exps_out[pair, unit, image] = exps
            mixed = dot(exps, jnp.concatenate([both_halves(value, keep), counts], axis=1), NN)
            inverse = 1.0 / mixed[:, 128:]
            at = slice(unit * 128, unit * 128 + 128)
            inv_out[pair, rows, at] = inverse
            ctx_out[pair, rows, at] = (mixed[:, :128] * inverse).astype(BF16)


def pack_kernel(chunks, place, w_qkv, w_out, w_fc1, fc2_t, own, both, later, qkv, out, sems):
    moves = [(w_qkv, qkv), (w_out, out)]
    start = 0
    for index, chunk in enumerate(chunks):
        target, at = (both, 768) if index == 1 else (later, index * chunk)
        for offset, weight in ((0, w_fc1), (chunk, fc2_t)):
            goal = target.at[:, at + offset : at + offset + chunk]
            moves.append((weight.at[:, start : start + chunk], goal))
        start += chunk
    copies = [
        pltpu.make_async_copy(source, goal, sems.at[index])
        for index, (source, goal) in enumerate(moves)
    ]
    for copy in copies:
        copy.start()
    for copy in copies[:2]:
        copy.wait()
    core = place[3]
    out_t = out[...].T
    for at, value in enumerate((qkv[0], qkv[1], qkv[2], out_t)):
        own[:, at * 128 : at * 128 + 128] = value[:, :128]
    pairs = ((qkv[0][:, 128:], qkv[2][:, 128:]), (qkv[1][:, 128:], out_t[:, 128:]))
    for at, (left, right) in enumerate(pairs):
        straight = jnp.concatenate([left, right], axis=1)
        turned = jnp.concatenate([right, left], axis=1)
        own[:, 512 + at * 128 : 640 + at * 128] = jnp.where(core == 0, straight, turned)
    both[:, :768] = own[...]
    for copy in copies[2:]:
        copy.wait()


def token_kernel(images, *refs):
    place, lengths, tokens, prompts, key_mask, grads, gain, shift = refs[:8]
    stream, normed, grad, visible, rows_f32 = refs[8:]
    position = lax.broadcasted_iota(jnp.int32, (SEQ, 1), 0)
    lane = lax.broadcasted_iota(jnp.int32, (1, SEQ), 1)
    for image in range(images):
        own = place[4] + image
        length = lengths[own]
        base = image * ROWS
        rows_f32[:IMG_TOK] = tokens[image].astype(F32)
        rows_f32[IMG_TOK:SEQ] = prompts[...].astype(F32)
        rows_f32[SEQ:] = jnp.zeros((ROWS - SEQ, rows_f32.shape[1]), F32)
        for start in (0, 152):
            rows = rows_f32[start : start + 152]
            stream[base + start : base + start + 152] = rows.astype(BF16)
            made = normalized(rows)[0] * gain[...] + shift[...]
            normed[base + start : base + start + 152] = made.astype(BF16)
        grad[base + ROWS - 16 : base + ROWS] = jnp.zeros((16, grad.shape[1]), BF16)
        used = position < IMG_TOK + length
        value = grads[image].astype(F32)
        grad[base : base + SEQ] = jnp.where(used, value, 0.0).astype(BF16)
        seen = (key_mask[pl.ds(own, 1)] == 1) | (lane == 0)
        visible[image] = jnp.zeros((1, KEYS), F32)
        visible[image, :, :SEQ] = (seen & (lane < IMG_TOK + length)).astype(F32)


def attend_kernel(loader, images, *refs):
    place, normed, visible, stream, b_out, gain, shift = refs[:7]
    pieces, refs = refs[7 : 7 + loader.count], refs[7 + loader.count :]
    qkv_out, exps_out, ctx_out, inv_out, mid_out, normed_out, wide, out, raw = refs
    loader.run(place, pieces, put_attn(wide, out, raw))
    for dy in range(2):
        join_thirds(raw, dy, wide.at[2], out.at[:, 512:])

    @pl.loop(0, 3)
    def _(pair):
        attend_units(
            images, pair, normed, wide[pair], visible, qkv_out, exps_out, ctx_out, inv_out
        )

    joined = jnp.concatenate([ctx_out[0], ctx_out[1], ctx_out[2]], axis=1)
    mid_out[...] = dot(joined, out[...], NT)

    def finish(rows):
        mid = stream[rows].astype(F32) + mid_out[rows] + b_out[...]
        mid_out[rows] = mid
        normed_out[rows] = (normalized(mid)[0] * gain[...] + shift[...]).astype(BF16)

    by_blocks(images * ROWS, 304, finish)


def gelu_parts(pre):
    density = jnp.exp(pre * pre * -0.5) * 0.3989422804014327
    chance = 0.5 + 0.5 * lax.erf(pre * 0.7071067811865476)
    return chance, density


def mlp_kernel(loader, chunk, slots, first, *refs):
    place, normed, grad, bias = refs[:4]
    refs = refs[4:]
    refs = refs if first else refs[2:]
    pieces = refs[: loader.count]
    out_sum, back_sum, up, down = refs[loader.count :]
    loader.run(place, pieces, put_mlp(up, down, chunk, slots))
    if first:
        out_sum[...] = jnp.zeros_like(out_sum)
        back_sum[...] = jnp.zeros_like(back_sum)
    half = normed.shape[0] // 2
    step = 1024

    @pl.loop(0, up.shape[1] // step)
    def _(index):
        cols = lanes_at(index * step, step)
        for part in range(2):
            rows = slice(part * half, (part + 1) * half)
            pre = dot(normed[rows], up[:, cols], NN) + bias[:, cols]
            grad_active = dot(grad[rows], down[:, cols], NN)
            chance, density = gelu_parts(pre)
            active = (pre * chance).astype(BF16)
            grad_pre = (grad_active * (chance + pre * density)).astype(BF16)
            out_sum[rows] += dot(active, down[:, cols], NT)
            back_sum[rows] += dot(grad_pre, up[:, cols], NT)


LATE = 192


def row_groups(images, late):
    start, stop = (LATE, ROWS) if late else (0, LATE)
    return [slice(image * ROWS + start, image * ROWS + stop) for image in range(images)]


def stream_grad(images, late, stacked, weights, stream, grad_mid, gain, body):
    for image, rows in enumerate(row_groups(images, late)):
        grads = stacked[rows]
        total = dot(grads[:, :768], weights[0], NT) + dot(grads[:, 768:1536], weights[1], NT)
        total = total + dot(grads[:, 1536:], weights[2], NT)
        unit, scale = normalized(stream[rows].astype(F32))
        body(image, grad_mid[rows] + norm_back(total, gain[...], unit, scale))


def back_kernel(images, *refs):
    place, mid, grad_normed, grad, stream, qkv, exps, context, inverse = refs[:9]
    gain_two, gain_one, wide, out = refs[9:13]
    keep_out, give_out, edge, grad_mid, stacked, grad_attn, grad_ctx = refs[13:]

    def begin(rows):
        unit, scale = normalized(mid[rows])
        back = grad[rows].astype(F32) + norm_back(grad_normed[rows], gain_two[...], unit, scale)
        grad_mid[rows] = back
        grad_attn[rows] = back.astype(BF16)

    by_blocks(images * ROWS, 304, begin)
    gradient = dot(grad_attn[...], out[...], NN)
    for index in range(3):
        grad_ctx[index] = gradient[:, index * 256 : index * 256 + 256]

    @pl.loop(0, 3)
    def _(pair):
        low = low_lanes(KEYS)
        keep = jnp.logical_xor(low, pair == 2)
        for image in range(images):
            rows = slice(image * ROWS, (image + 1) * ROWS)
            for unit in range(2):
                at = slice(unit * 128, unit * 128 + 128)
                scaled = (grad_ctx[pair, rows, at] * inverse[pair, rows, at]).astype(BF16)
                product = scaled.astype(F32) * context[pair, rows, at].astype(F32)
                query = qkv[pair, unit, image, :ROWS, :128]
                keys = both_halves(
                    qkv[pair, unit, image, :, 128:256] * jnp.asarray(0.125, BF16), low
                )
                values = both_halves(qkv[pair, unit, image, :, 256:], keep)
                grad_probs = dot(scaled, values, NT)
                parts = []
                for head in range(2):
                    lanes = slice(head * KEYS, (head + 1) * KEYS)
                    own = keep[:ROWS] if head == 0 else jnp.logical_not(keep[:ROWS])
                    delta = jnp.sum(jnp.where(own, product, 0.0), axis=-1, keepdims=True)
                    weight = exps[pair, unit, image, :, lanes].astype(F32)
                    parts.append((weight * (grad_probs[:, lanes] - delta)).astype(BF16))
                grad_scores = jnp.concatenate(parts, axis=1)
                weights = side_to_rows(exps[pair, unit, image])
                made = (
                    dot(grad_scores, keys, NN),
                    dot(side_to_rows(grad_scores), both_halves(query, low[:ROWS]), TN)[:ROWS],
                    dot(weights, both_halves(scaled, keep[:ROWS]), TN)[:ROWS],
                )
                for index, value in enumerate(made):
                    to = lanes_at(pair * 768 + unit * 384 + index * 128, 128)
                    stacked[rows, to] = value.astype(BF16)

    sums = []

    def finish(image, back):
        edge[image] = back[: IMG_TOK - LATE]
        sums.append(back[IMG_TOK - LATE : SEQ - LATE])

    stream_grad(images, True, stacked, wide, stream, grad_mid, gain_one, finish)
    prompt_sum = functools.reduce(jnp.add, sums)
    half = prompt_sum.shape[1] // 2
    low, high = prompt_sum[:, :half], prompt_sum[:, half:]
    keep_low = (place[3] == 0) | (give_out.dtype == F32)
    keep_out[...] = jnp.where(keep_low, low, high)
    give_out[...] = jnp.where(keep_low, high, low).astype(give_out.dtype)


def last_kernel(images, *refs):
    place, lengths, mid, mlp_out, stream, b_fc2, gain_one, wide = refs[:8]
    edge, grad_mid, stacked, result, grad_input = refs[8:]
    width = mid.shape[1]
    position = lax.broadcasted_iota(jnp.int32, (ROWS, 1), 0)
    for image in range(images):
        rows = slice(image * ROWS, (image + 1) * ROWS)
        used = (position < IMG_TOK + lengths[place[4] + image]).astype(F32)
        rows_out = (mid[rows] + mlp_out[rows] + b_fc2[...]) * used
        result[:, image * width : (image + 1) * width] = rows_out[:SEQ].astype(BF16)

    def finish(image, back):
        lanes = slice(image * width, (image + 1) * width)
        grad_input[:LATE, lanes] = back.astype(BF16)
        grad_input[LATE:, lanes] = edge[image].astype(BF16)

    stream_grad(images, False, stacked, wide, stream, grad_mid, gain_one, finish)


SMEM = pl.BlockSpec(memory_space=pltpu.SMEM)
VMEM = pl.BlockSpec(memory_space=pltpu.VMEM)
ANY = pl.BlockSpec(memory_space=pl.ANY)
HBM = pl.BlockSpec(memory_space=pltpu.HBM)


def cost(flops, nbytes):
    return pl.CostEstimate(
        flops=int(flops * COST_SCALE), bytes_accessed=int(nbytes * COST_SCALE), transcendentals=0
    )


def call(kernel, outs, scratch, estimate, scalars, operands, grant, aliases=None, waits=()):
    ahead = len(scalars) + len(operands)
    skip = lambda *refs: kernel(*refs[:ahead], *refs[ahead + len(waits) :])
    return pl.pallas_call(
        skip,
        in_specs=[SMEM] * len(scalars) + [VMEM] * len(operands) + [ANY] * len(waits),
        out_specs=[VMEM] * len(outs),
        out_shape=[jax.ShapeDtypeStruct(shape, kind) for shape, kind in outs],
        scratch_shapes=[pltpu.VMEM(shape, kind) for shape, kind in scratch],
        compiler_params=pltpu.CompilerParams(vmem_limit_bytes=grant << 20),
        cost_estimate=estimate,
        input_output_aliases=aliases or {},
    )(*scalars, *operands, *waits)


def saved_shapes(images, rows):
    return [
        ((3, 2, images, KEYS, 384), BF16),
        ((3, 2, images, ROWS, 2 * KEYS), BF16),
        ((3, rows, 256), BF16),
        ((3, rows, 256), F32),
    ]


def pack_weights(chunks, place, w_qkv, w_out, w_fc1, w_fc2):
    rows = w_fc1.shape[0]
    shapes = (rows, 768), (rows, 768 + 2 * chunks[1]), (rows, 2 * (chunks[0] + chunks[2]))
    return pl.pallas_call(
        functools.partial(pack_kernel, chunks),
        in_specs=[SMEM] + [HBM] * 4,
        out_specs=[VMEM] * 3,
        out_shape=[jax.ShapeDtypeStruct(shape, BF16) for shape in shapes],
        scratch_shapes=[
            pltpu.VMEM(w_qkv.shape, BF16),
            pltpu.VMEM(w_out.shape, BF16),
            pltpu.SemaphoreType.DMA((2 + 2 * len(chunks),)),
        ],
        compiler_params=pltpu.CompilerParams(vmem_limit_bytes=63 << 20),
        cost_estimate=cost(1e7, 1e7),
    )(place, w_qkv, w_out, w_fc1, w_fc2.T)


def prepare_tokens(place, lengths, tokens, prompts, key_mask, grads, gain, shift):
    images, _, width = tokens.shape
    rows = images * ROWS
    return call(
        functools.partial(token_kernel, images),
        [((rows, width), BF16)] * 3 + [((images, 1, KEYS), F32)],
        [((ROWS, width), F32)],
        cost(1e7, 1e7),
        (place, lengths),
        (tokens, prompts, key_mask, grads, gain, shift),
        4,
    )


def attend(loader, images, place, normed, visible, stream, b_out, gain, shift, pieces, waits):
    rows, width = normed.shape
    return call(
        functools.partial(attend_kernel, loader, images),
        saved_shapes(images, rows)
        + [((rows, width), F32), ((rows, width), BF16)]
        + [((3, width, 768), BF16), ((width, 768), BF16)],
        [((width, 1024), BF16)],
        cost(8e9, 1e7),
        (place,),
        (normed, visible, stream, b_out, gain, shift, *pieces),
        GRANTS[0],
        waits=waits,
    )


def mlp(loader, slots, place, normed, grad, bias, sums, pieces, waits):
    rows, width = normed.shape
    hidden = bias.shape[1]
    first = sums is None
    sums = () if first else tuple(sums)
    return call(
        functools.partial(mlp_kernel, loader, hidden // slots, slots, first),
        [((rows, width), F32)] * 2,
        [((width, hidden), BF16)] * 2,
        cost(8.0 * rows * width * hidden, 1.6e7),
        (place,),
        (normed, grad, bias, *sums, *pieces),
        GRANTS[2],
        {} if first else {4: 0, 5: 1},
        waits,
    )


def attend_back(
    images, give_kind, place, mid, grad_normed, grad, stream, saved, gain_two, gain_one, weights
):
    rows, width = mid.shape
    return call(
        functools.partial(back_kernel, images),
        [
            ((PROMPTS, width // 2), F32),
            ((PROMPTS, width // 2), give_kind),
            ((images, IMG_TOK - LATE, width), F32),
            ((rows, width), F32),
            ((rows, 3 * 768), BF16),
        ],
        [((rows, width), BF16), ((3, rows, 256), F32)],
        cost(9e9, 2.4e7),
        (place,),
        (mid, grad_normed, grad, stream, *saved, gain_two, gain_one, *weights),
        GRANTS[3],
    )


def finish_rows(images, place, lengths, mid, mlp_out, stream, b_fc2, gain_one, weights, passed):
    width = mid.shape[1]
    return call(
        functools.partial(last_kernel, images),
        [((SEQ, images * width), BF16), ((IMG_TOK, images * width), BF16)],
        [],
        cost(2e9, 1e7),
        (place, lengths),
        (mid, mlp_out, stream, b_fc2, gain_one, weights[0], *passed),
        7,
    )


def add_kernel(*refs):
    *parts, out = refs
    parts = [part[...].astype(F32) for part in parts]
    while len(parts) > 1:
        parts = [parts[at] + parts[at + 1] for at in range(0, len(parts), 2)]
    out[...] = parts[0].astype(BF16)


def add(*parts, waits=()):
    outs = [(parts[-1].shape, BF16)]
    return call(add_kernel, outs, [], cost(0, 0), (), parts, 1, waits=waits)[0]


def sum_prompts(exchange, keep, give, results):
    mine = add(keep, exchange.core(give))
    others = [exchange.swap(mine, dx=dx, dy=dy) for dx, dy in ((1, 0), (0, 1), (1, 1))]
    mine = add(mine, *others, waits=results)
    for dz in (1, 2):
        mine = add(mine, exchange.swap(mine, dz=dz))
    other = exchange.core(mine).astype(F32)
    mine = lax.reduce_precision(mine.astype(F32), 8, 7)
    return jnp.where(
        lax.axis_index("head") % 2 == 0,
        jnp.concatenate([mine, other], axis=1),
        jnp.concatenate([other, mine], axis=1),
    )


def per_device(
    exchange,
    layer_input,
    prompts,
    lengths,
    key_mask,
    ln1_gain,
    ln1_shift,
    w_qkv,
    w_out,
    b_out,
    ln2_gain,
    ln2_shift,
    w_fc1,
    b_fc1,
    w_fc2,
    b_fc2,
    grad_output,
):
    images, _, width = layer_input.shape
    chunks = CHUNKS
    head = lax.axis_index("head")
    core = head % 2

    if exchange is not None:
        depth = exchange.depth
        dp = lax.axis_index("dp")
        place = [dp // 2, dp % 2, head // 2, core]
    else:
        depth = 0
        place = [0, 0, 0, core]
    place = jnp.stack([jnp.asarray(value, jnp.int32) for value in (*place, head * images)])

    own, both, later = pack_weights(chunks, place, w_qkv, w_out, w_fc1, w_fc2)
    if exchange is not None:
        gather = Gather(exchange, own, both, later, b_fc1)
    else:

        def gather_whole(piece):
            rows = lax.all_gather(piece, "dp", axis=0, tiled=True)
            held = Held(None)
            held.arrays = [lax.all_gather(rows, "head", axis=0)]
            held.plan = [(0, ALL, [(dy, c) for dy in (0, 1) for c in (0, 1)])]
            return held

        attn = gather_whole(own)
        split = 2 * chunks[0]
        gathered = [gather_whole(piece) for piece in (later[:, :split], both[:, 768:], later[:, split:])]
        bias = lax.all_gather(b_fc1, "head", axis=0)

    row = lambda vector: vector.reshape(1, -1)
    stream, normed, grad, visible = prepare_tokens(
        place, lengths, layer_input, prompts, key_mask, grad_output, row(ln1_gain), row(ln1_shift)
    )
    waits = ()
    if exchange is not None:
        attn, (normed, visible, stream, grad) = gather.attention(normed, visible, stream, grad)
        bias = gather.bias
        waits = (bias,)
    load_attn = Loader(attn.plan, depth)
    *saved, mid, normed_mlp, wide, out = attend(
        load_attn, images, place, normed, visible, stream,
        row(b_out), row(ln2_gain), row(ln2_shift), attn.arrays, waits,
    )
    if exchange is None:
        order = [(bias, gathered[index], 4, index) for index in range(3)]
    else:
        normed_mlp = gather.round_seven(normed_mlp)
        even, odd = bias[0::2], bias[1::2]
        biases = jnp.where(core == 0, even, odd), jnp.where(core == 0, odd, even)
        both = Held(None)
        both.arrays = gather.halves[0].arrays + gather.halves[1].arrays
        both.plan = gather.halves[0].plan + gather.halves[1].plan
        order = [(bias, both, 4, 0)]
        order += [(bias, gather.parts[index], 4, index) for index in (1, 2)]
    sums = None
    for values, held, slots, index in order:
        if exchange is not None and index == 1:
            sums[0] = gather.round_eight(sums[0])
        chunk_bias = row(values[:, sum(chunks[:index]) : sum(chunks[: index + 1])])
        loader = Loader(held.plan, depth)
        sums = mlp(loader, slots, place, normed_mlp, grad, chunk_bias, sums, held.arrays, ())
        sums = list(sums)
    weights = (wide, out)
    keep, give, *passed = attend_back(
        images, BF16 if exchange is not None else F32, place, mid, sums[1], grad, stream, saved,
        row(ln2_gain), row(ln1_gain), weights,
    )
    results = finish_rows(
        images, place, lengths, mid, sums[0], stream, row(b_fc2), row(ln1_gain), weights, passed
    )
    if exchange is not None:
        total = sum_prompts(exchange, keep, give, results)
    else:
        total = lax.psum(jnp.concatenate([keep, give], axis=1), BOTH)
    results = [result.reshape(result.shape[0], images, width) for result in results]
    return (*(jnp.transpose(result, (1, 0, 2)) for result in results), total)


def solution(mesh):
    dp, head = mesh.shape["dp"], mesh.shape["head"]
    exchange = Exchange(dp, head) if (dp, head) == (8, 4) else None
    placed = (
        P(BOTH, None, None),
        P(),
        P("dp"),
        P("dp", None),
        P(),
        P(),
        P(None, "dp", "head"),
        P("head", "dp"),
        P(),
        P(),
        P(),
        P("dp", "head"),
        P("head"),
        P("head", "dp"),
        P(),
        P(BOTH, None, None),
    )
    return jax.shard_map(
        functools.partial(per_device, exchange),
        mesh=mesh,
        in_specs=placed,
        out_specs=(P(BOTH, None, None), P(BOTH, None, None), P()),
        check_vma=False,
    )
```

```python
import functools

import jax
import jax.numpy as jnp
from jax import lax
from jax.experimental import pallas as pl
from jax.experimental.pallas import tpu as pltpu
from jax.sharding import PartitionSpec as P

HEAD_DIM = 64
IMG_TOK = 197
PROMPTS = 100
SEQ = IMG_TOK + PROMPTS
ROWS = 304
KEYS = 384
EPSILON = 1e-06
GRANTS = (9, 9, 9, 11)
COST_SCALE = 10.0
CHUNKS = (256, 256, 256)
BOTH = ("dp", "head")
F32 = jnp.float32
BF16 = jnp.bfloat16

NN = (((1,), (0,)), ((), ()))
NT = (((1,), (1,)), ((), ()))
TN = (((0,), (0,)), ((), ()))


def dot(left, right, dims):
    return lax.dot_general(left, right, dims, preferred_element_type=F32)


def device_perm(count, target):
    pairs = []
    for index in range(count):
        c, y, x, z = index % 2, index // 2 % 2, index // 4 % 2, index // 8
        z, x, y, c = target(z, x, y, c)
        pairs.append((index, ((z * 2 + x) * 2 + y) * 2 + c))
    return pairs


def along_ring(z, step, depth):
    place = ((z ^ (z >> 1)) + step + depth) % depth
    return place ^ (place >> 1)


class Exchange:
    def __init__(self, dp, head):
        self.count = dp * head
        self.depth = dp // 2

    def move(self, value, target):
        return lax.ppermute(value, BOTH, device_perm(self.count, target))

    def from_z(self, value, step):
        return self.move(value, lambda z, x, y, c: (along_ring(z, -step, self.depth), x, y, c))

    def first(self, value):
        return self.move(value, lambda z, x, y, c: (z, x ^ (1 - c), y ^ c, c))

    def second(self, value):
        return self.move(value, lambda z, x, y, c: (z, x ^ c, y ^ (1 - c), c))

    def core(self, value):
        return self.move(value, lambda z, x, y, c: (z, x, y, 1 - c))

    def swap(self, value, dz=0, dx=0, dy=0):
        return self.move(value, lambda z, x, y, c: (z ^ dz, x ^ dx, y ^ dy, c))


def tie(*values):
    return lax.optimization_barrier(values)


ALL, UP, DOWN = range(3)
NEAR_FAR = ((0, 0), (1, 0), (0, 1), (1, 1))


class Held:
    def __init__(self, exchange):
        self.exchange = exchange
        self.arrays, self.plan = [], []

    def add(self, array, lane, steps, halves, is_other=0, kind=ALL):
        self.arrays.append(array)
        entries = [(step, half, is_far, is_other) for half, is_far in halves for step in steps]
        self.plan.append((lane, kind, entries))

    def add_both(self, array, steps, halves):
        self.add(array, 0, steps, halves, 0)
        self.add(self.exchange.core(array), 0, steps, halves, 1)

    def add_pair(self, pair, lane, steps, halves, kind=ALL):
        for is_other, array in enumerate(pair):
            self.add(array, lane, steps, halves, is_other, kind)


class Gather:
    def __init__(self, exchange, own, both, later, bias):
        self.exchange, self.width, self.part = exchange, own.shape[1], later.shape[1] // 2
        own, both, self.later, self.bias = own[None], both[None], later[None], bias
        first = exchange.first(both)
        self.came = jnp.concatenate([exchange.from_z(own, 1), exchange.from_z(own, 3)])
        self.own = both, first

    def attention(self, *ready):
        exchange, width, part = self.exchange, self.width, self.part
        both, first, came, later, bias = tie(*self.own, self.came, self.later, self.bias)
        near = jnp.concatenate([both, first])
        own_far = exchange.second(near)
        two = exchange.from_z(came[:1], 1)
        other = exchange.core(bias)
        at_low = lax.axis_index("head") % 2 == 0
        bias = jnp.where(at_low, jnp.stack([bias, other]), jnp.stack([other, bias]))
        own_near, own_far, base, later, bias, *ready = tie(
            near, own_far, jnp.concatenate([came, two]), later, bias, *ready
        )
        first = exchange.first(base)
        later_one = exchange.from_z(later, 1)
        owns = (own_near, own_far, exchange.core(own_near), exchange.core(own_far))
        near, later_one, later, bias, *owns = tie(
            jnp.concatenate([base, first]), later_one, later, bias, *owns
        )
        far = exchange.second(near)
        later_three = exchange.from_z(later, 3)
        later_two = exchange.from_z(later_one, 1)
        other_near = exchange.core(near)
        self.bias = jnp.concatenate([bias, exchange.swap(bias, dy=1)])
        far, base, self.plane, self.bias = tie(
            far,
            jnp.concatenate([later, later_one, later_three, later_two]),
            jnp.concatenate([owns[0][:, :, width:], owns[1][:, :, width:]]),
            self.bias,
        )
        near_later = jnp.concatenate([base, exchange.first(base)])
        self.up = exchange.from_z(self.plane, 1)
        self.later_near, self.up, self.plane = tie(near_later, self.up, self.plane)
        self.split = part + part // 2
        self.later_far = exchange.second(self.later_near[:, :, : self.split])
        self.other_near = exchange.core(self.later_near)
        self.down = exchange.from_z(self.plane, 3)
        self.low = exchange.from_z(self.up[:2], 1)

        held = Held(exchange)
        self.parts = [Held(exchange) for _ in range(3)]
        for index, array in enumerate(owns):
            halves = NEAR_FAR[2 * (index % 2) : 2 * (index % 2) + 2]
            held.add(array, 0, (0,), halves, index // 2)
            self.parts[1].add(array, width, (0,), halves, index // 2)
        held.add(near, 0, (1, 3, 2), NEAR_FAR[:2], 0)
        held.add(other_near, 0, (1, 3, 2), NEAR_FAR[:2], 1)
        held.add_both(far, (1, 3, 2), NEAR_FAR[2:])
        return held, ready

    def round_seven(self, token):
        exchange, steps = self.exchange, (0, 1, 3, 2)
        near, far, up, down, low, token = tie(
            self.later_near, self.later_far, self.up, self.down, self.low, token
        )
        self.rest = exchange.second(near[:, :, self.split :])
        self.high = exchange.from_z(down[2:], 3)
        near, far = (near, self.other_near), (far, exchange.core(far))
        self.parts[2].add_pair(near, self.part, steps, NEAR_FAR[:2])
        self.parts[2].add_pair(far, self.part, steps, NEAR_FAR[2:], UP)
        self.halves = [Held(exchange), Held(exchange)]
        for is_other, held in enumerate(self.halves):
            held.add(near[is_other], 0, steps, NEAR_FAR[:2], is_other)
            held.add(far[is_other], 0, steps, NEAR_FAR[2:], is_other)
        self.parts[1].add_both(up, (1,), NEAR_FAR)
        self.parts[1].add_both(down, (3,), NEAR_FAR)
        self.parts[1].add_both(low, (2,), NEAR_FAR[:2])
        return token

    def round_eight(self, token):
        high, rest, token = tie(self.high, self.rest, token)
        self.parts[1].add_both(high, (2,), NEAR_FAR[2:])
        self.parts[2].add_pair((rest, self.exchange.core(rest)), 0, (0, 1, 3, 2), NEAR_FAR[2:], DOWN)
        return token


def placement(entry, place, depth):
    z, x, y, c = place
    step, half, is_far, is_other = entry
    core = 1 - c if is_other else c
    dx = jnp.where(core == 0, half, is_far)
    dy = jnp.where(core == 0, is_far, half)
    block = along_ring(z, step, depth) * 2 + jnp.where(dx == 1, 1 - x, x)
    return block, dy, core


def row_mean(value):
    return jnp.mean(value, axis=-1, keepdims=True)


def normalized(rows):
    center = rows - row_mean(rows)
    scale = lax.rsqrt(row_mean(center * center) + EPSILON)
    return center * scale, scale


def norm_back(grad, gain, unit, scale):
    grad = grad * gain
    return scale * (grad - row_mean(grad) - unit * row_mean(grad * unit))


def low_lanes(rows):
    return lax.broadcasted_iota(jnp.int32, (rows, 128), 1) < HEAD_DIM


def both_halves(tile, keep):
    zero = jnp.zeros_like(tile)
    return jnp.concatenate([jnp.where(keep, tile, zero), jnp.where(keep, zero, tile)], axis=0)


def side_to_rows(pair):
    return jnp.concatenate([pair[:, :KEYS], pair[:, KEYS:]], axis=0)


def by_blocks(rows, size, body):
    @pl.loop(0, rows // size)
    def _(index):
        body(pl.ds(pl.multiple_of(index * size, size), size))


class Loader:
    def __init__(self, plan, depth):
        self.plan, self.depth = plan, depth
        self.count = len(plan)

    def run(self, place_ref, pieces, put):
        place = tuple(place_ref[i] for i in range(4))
        for ref, (lane, kind, entries) in zip(pieces, self.plan):
            for index, entry in enumerate(entries):
                rows = ref.shape[1]
                if self.depth:
                    block, dy, core = placement(entry, place, self.depth)
                    where = pl.ds(pl.multiple_of(block * rows, rows), rows)
                else:
                    (dy, core), where = entry, pl.ds(0, rows)
                put(ref.at[index, :, lane:], where, dy, core, kind)


def lanes_at(start, size):
    return pl.ds(pl.multiple_of(start, 128), size)


def put_attn(wide, out, raw):
    def put(source, rows, dy, core, kind):
        slot = dy * 2 + core
        wide[dy, rows, lanes_at(core * 384, 384)] = source[:, :384]
        out[rows, lanes_at(slot * 128, 128)] = source[:, 384:512]
        raw[rows, lanes_at(slot * 256, 256)] = source[:, 512:768]

    return put


def join_thirds(raw, dy, wide, out):
    even, odd = raw[:, dy * 512 : dy * 512 + 256], raw[:, dy * 512 + 256 : dy * 512 + 512]
    low = low_lanes(even.shape[0])
    at = dy * 384
    wide[:, at : at + 128] = jnp.where(low, even[:, :128], odd[:, :128])
    wide[:, at + 128 : at + 256] = jnp.where(low, even[:, 128:], odd[:, 128:])
    wide[:, at + 256 : at + 384] = jnp.where(low, odd[:, :128], even[:, :128])
    out[:, dy * 128 : dy * 128 + 128] = jnp.where(low, odd[:, 128:], even[:, 128:])


def put_mlp(up, down, chunk, slots):
    def put(source, rows, dy, core, kind):
        lanes = lanes_at((dy if slots == 2 else dy * 2 + core) * chunk, chunk)
        if kind != DOWN:
            up[rows, lanes] = source[:, :chunk]
        if kind != UP:
            start = 0 if kind == DOWN else chunk
            down[rows, lanes] = source[:, start : start + chunk]

    return put


def attend_units(images, pair, normed, weights, visible, qkv_out, exps_out, ctx_out, inv_out):
    qkv = dot(normed[...], weights, NN)
    low = low_lanes(KEYS)
    keep = jnp.logical_xor(low, pair == 2)
    counts = both_halves(jnp.ones((KEYS, 128), BF16), keep)
    padding = jnp.zeros((KEYS - ROWS, 128), BF16)
    for image in range(images):
        rows = slice(image * ROWS, (image + 1) * ROWS)
        see = visible[image] > 0
        for unit in range(2):
            tiles = [qkv[rows, unit * 384 + at : unit * 384 + at + 128] for at in (0, 128, 256)]
            query = (tiles[0] * 0.125).astype(BF16)
            key, value = (
                jnp.concatenate([tile.astype(BF16), padding], axis=0) for tile in tiles[1:]
            )
            qkv_out[pair, unit, image, :ROWS, :128] = query
            qkv_out[pair, unit, image, :, 128:256] = key
            qkv_out[pair, unit, image, :, 256:] = value
            scores = dot(query, both_halves(key, low), NT)
            parts = []
            for head in range(2):
                part = jnp.where(see, scores[:, head * KEYS : (head + 1) * KEYS], -1000000000.0)
                part = jnp.exp(part - jnp.max(part, axis=-1, keepdims=True))
                parts.append(part.astype(BF16))
            exps = jnp.concatenate(parts, axis=1)
            exps_out[pair, unit, image] = exps
            mixed = dot(exps, jnp.concatenate([both_halves(value, keep), counts], axis=1), NN)
            inverse = 1.0 / mixed[:, 128:]
            at = slice(unit * 128, unit * 128 + 128)
            inv_out[pair, rows, at] = inverse
            ctx_out[pair, rows, at] = (mixed[:, :128] * inverse).astype(BF16)


def pack_kernel(chunks, place, w_qkv, w_out, w_fc1, fc2_t, own, both, later, qkv, out, sems):
    moves = [(w_qkv, qkv), (w_out, out)]
    start = 0
    for index, chunk in enumerate(chunks):
        target, at = (both, 768) if index == 1 else (later, index * chunk)
        for offset, weight in ((0, w_fc1), (chunk, fc2_t)):
            goal = target.at[:, at + offset : at + offset + chunk]
            moves.append((weight.at[:, start : start + chunk], goal))
        start += chunk
    copies = [
        pltpu.make_async_copy(source, goal, sems.at[index])
        for index, (source, goal) in enumerate(moves)
    ]
    for copy in copies:
        copy.start()
    for copy in copies[:2]:
        copy.wait()
    core = place[3]
    out_t = out[...].T
    for at, value in enumerate((qkv[0], qkv[1], qkv[2], out_t)):
        own[:, at * 128 : at * 128 + 128] = value[:, :128]
    pairs = ((qkv[0][:, 128:], qkv[2][:, 128:]), (qkv[1][:, 128:], out_t[:, 128:]))
    for at, (left, right) in enumerate(pairs):
        straight = jnp.concatenate([left, right], axis=1)
        turned = jnp.concatenate([right, left], axis=1)
        own[:, 512 + at * 128 : 640 + at * 128] = jnp.where(core == 0, straight, turned)
    both[:, :768] = own[...]
    for copy in copies[2:]:
        copy.wait()


def token_kernel(images, *refs):
    place, lengths, tokens, prompts, key_mask, grads, gain, shift = refs[:8]
    stream, normed, grad, visible, rows_f32 = refs[8:]
    position = lax.broadcasted_iota(jnp.int32, (SEQ, 1), 0)
    lane = lax.broadcasted_iota(jnp.int32, (1, SEQ), 1)
    for image in range(images):
        own = place[4] + image
        length = lengths[own]
        base = image * ROWS
        rows_f32[:IMG_TOK] = tokens[image].astype(F32)
        rows_f32[IMG_TOK:SEQ] = prompts[...].astype(F32)
        rows_f32[SEQ:] = jnp.zeros((ROWS - SEQ, rows_f32.shape[1]), F32)
        for start in (0, 152):
            rows = rows_f32[start : start + 152]
            stream[base + start : base + start + 152] = rows.astype(BF16)
            made = normalized(rows)[0] * gain[...] + shift[...]
            normed[base + start : base + start + 152] = made.astype(BF16)
        grad[base + ROWS - 16 : base + ROWS] = jnp.zeros((16, grad.shape[1]), BF16)
        used = position < IMG_TOK + length
        value = grads[image].astype(F32)
        grad[base : base + SEQ] = jnp.where(used, value, 0.0).astype(BF16)
        seen = (key_mask[pl.ds(own, 1)] == 1) | (lane == 0)
        visible[image] = jnp.zeros((1, KEYS), F32)
        visible[image, :, :SEQ] = (seen & (lane < IMG_TOK + length)).astype(F32)


def attend_kernel(loader, images, *refs):
    place, normed, visible, stream, b_out, gain, shift = refs[:7]
    pieces, refs = refs[7 : 7 + loader.count], refs[7 + loader.count :]
    qkv_out, exps_out, ctx_out, inv_out, mid_out, normed_out, wide, out, raw = refs
    loader.run(place, pieces, put_attn(wide, out, raw))
    for dy in range(2):
        join_thirds(raw, dy, wide.at[2], out.at[:, 512:])

    @pl.loop(0, 3)
    def _(pair):
        attend_units(
            images, pair, normed, wide[pair], visible, qkv_out, exps_out, ctx_out, inv_out
        )

    joined = jnp.concatenate([ctx_out[0], ctx_out[1], ctx_out[2]], axis=1)
    mid_out[...] = dot(joined, out[...], NT)

    def finish(rows):
        mid = stream[rows].astype(F32) + mid_out[rows] + b_out[...]
        mid_out[rows] = mid
        normed_out[rows] = (normalized(mid)[0] * gain[...] + shift[...]).astype(BF16)

    by_blocks(images * ROWS, 304, finish)


def gelu_parts(pre):
    density = jnp.exp(pre * pre * -0.5) * 0.3989422804014327
    chance = 0.5 + 0.5 * lax.erf(pre * 0.7071067811865476)
    return chance, density


def mlp_kernel(loader, chunk, slots, first, *refs):
    place, normed, grad, bias = refs[:4]
    refs = refs[4:]
    sums_in, refs = (None, refs) if first else (refs[:2], refs[2:])
    pieces = refs[: loader.count]
    out_sum, back_sum, up, down = refs[loader.count :]
    loader.run(place, pieces, put_mlp(up, down, chunk, slots))
    half = normed.shape[0] // 2
    step = 1024
    for start in range(0, up.shape[1], step):
        cols = slice(start, start + step)
        for part in range(2):
            rows = slice(part * half, (part + 1) * half)
            pre = dot(normed[rows], up[:, cols], NN) + bias[:, cols]
            grad_active = dot(grad[rows], down[:, cols], NN)
            chance, density = gelu_parts(pre)
            active = (pre * chance).astype(BF16)
            grad_pre = (grad_active * (chance + pre * density)).astype(BF16)
            made = dot(active, down[:, cols], NT), dot(grad_pre, up[:, cols], NT)
            held = sums_in if start == 0 else (out_sum, back_sum)
            for index, (total, value) in enumerate(zip((out_sum, back_sum), made)):
                total[rows] = value if held is None else held[index][rows] + value


def _(index):
        cols = lanes_at(index * step, step)
        for part in range(2):
            rows = slice(part * half, (part + 1) * half)
            pre = dot(normed[rows], up[:, cols], NN) + bias[:, cols]
            grad_active = dot(grad[rows], down[:, cols], NN)
            chance, density = gelu_parts(pre)
            active = (pre * chance).astype(BF16)
            grad_pre = (grad_active * (chance + pre * density)).astype(BF16)
            out_sum[rows] += dot(active, down[:, cols], NT)
            back_sum[rows] += dot(grad_pre, up[:, cols], NT)


LATE = 192


def row_groups(images, late):
    start, stop = (LATE, ROWS) if late else (0, LATE)
    return [slice(image * ROWS + start, image * ROWS + stop) for image in range(images)]


def stream_grad(images, late, stacked, weights, stream, grad_mid, gain, body):
    for image, rows in enumerate(row_groups(images, late)):
        grads = stacked[rows]
        total = dot(grads[:, :768], weights[0], NT) + dot(grads[:, 768:1536], weights[1], NT)
        total = total + dot(grads[:, 1536:], weights[2], NT)
        unit, scale = normalized(stream[rows].astype(F32))
        body(image, grad_mid[rows] + norm_back(total, gain[...], unit, scale))


def back_kernel(images, *refs):
    place, mid, grad_normed, grad, stream, qkv, exps, context, inverse = refs[:9]
    gain_two, gain_one, wide, out = refs[9:13]
    keep_out, give_out, edge, grad_mid, stacked, grad_attn, grad_ctx = refs[13:]

    def begin(rows):
        unit, scale = normalized(mid[rows])
        back = grad[rows].astype(F32) + norm_back(grad_normed[rows], gain_two[...], unit, scale)
        grad_mid[rows] = back
        grad_attn[rows] = back.astype(BF16)

    by_blocks(images * ROWS, 304, begin)
    gradient = dot(grad_attn[...], out[...], NN)
    for index in range(3):
        grad_ctx[index] = gradient[:, index * 256 : index * 256 + 256]

    @pl.loop(0, 3)
    def _(pair):
        low = low_lanes(KEYS)
        keep = jnp.logical_xor(low, pair == 2)
        for image in range(images):
            rows = slice(image * ROWS, (image + 1) * ROWS)
            for unit in range(2):
                at = slice(unit * 128, unit * 128 + 128)
                scaled = (grad_ctx[pair, rows, at] * inverse[pair, rows, at]).astype(BF16)
                product = scaled.astype(F32) * context[pair, rows, at].astype(F32)
                query = qkv[pair, unit, image, :ROWS, :128]
                keys = both_halves(
                    qkv[pair, unit, image, :, 128:256] * jnp.asarray(0.125, BF16), low
                )
                values = both_halves(qkv[pair, unit, image, :, 256:], keep)
                grad_probs = dot(scaled, values, NT)
                parts = []
                for head in range(2):
                    lanes = slice(head * KEYS, (head + 1) * KEYS)
                    own = keep[:ROWS] if head == 0 else jnp.logical_not(keep[:ROWS])
                    delta = jnp.sum(jnp.where(own, product, 0.0), axis=-1, keepdims=True)
                    weight = exps[pair, unit, image, :, lanes].astype(F32)
                    parts.append((weight * (grad_probs[:, lanes] - delta)).astype(BF16))
                grad_scores = jnp.concatenate(parts, axis=1)
                weights = side_to_rows(exps[pair, unit, image])
                made = (
                    dot(grad_scores, keys, NN),
                    dot(side_to_rows(grad_scores), both_halves(query, low[:ROWS]), TN)[:ROWS],
                    dot(weights, both_halves(scaled, keep[:ROWS]), TN)[:ROWS],
                )
                for index, value in enumerate(made):
                    to = lanes_at(pair * 768 + unit * 384 + index * 128, 128)
                    stacked[rows, to] = value.astype(BF16)

    sums = []

    def finish(image, back):
        edge[image] = back[: IMG_TOK - LATE]
        sums.append(back[IMG_TOK - LATE : SEQ - LATE])

    stream_grad(images, True, stacked, wide, stream, grad_mid, gain_one, finish)
    prompt_sum = functools.reduce(jnp.add, sums)
    half = prompt_sum.shape[1] // 2
    low, high = prompt_sum[:, :half], prompt_sum[:, half:]
    keep_low = (place[3] == 0) | (give_out.dtype == F32)
    keep_out[...] = jnp.where(keep_low, low, high)
    give_out[...] = jnp.where(keep_low, high, low).astype(give_out.dtype)


def last_kernel(images, *refs):
    place, lengths, mid, mlp_out, stream, b_fc2, gain_one, wide = refs[:8]
    edge, grad_mid, stacked, result, grad_input = refs[8:]
    width = mid.shape[1]
    position = lax.broadcasted_iota(jnp.int32, (ROWS, 1), 0)
    for image in range(images):
        rows = slice(image * ROWS, (image + 1) * ROWS)
        used = (position < IMG_TOK + lengths[place[4] + image]).astype(F32)
        rows_out = (mid[rows] + mlp_out[rows] + b_fc2[...]) * used
        result[:, image * width : (image + 1) * width] = rows_out[:SEQ].astype(BF16)

    def finish(image, back):
        lanes = slice(image * width, (image + 1) * width)
        grad_input[:LATE, lanes] = back.astype(BF16)
        grad_input[LATE:, lanes] = edge[image].astype(BF16)

    stream_grad(images, False, stacked, wide, stream, grad_mid, gain_one, finish)


SMEM = pl.BlockSpec(memory_space=pltpu.SMEM)
VMEM = pl.BlockSpec(memory_space=pltpu.VMEM)
ANY = pl.BlockSpec(memory_space=pl.ANY)
HBM = pl.BlockSpec(memory_space=pltpu.HBM)


def cost(flops, nbytes):
    return pl.CostEstimate(
        flops=int(flops * COST_SCALE), bytes_accessed=int(nbytes * COST_SCALE), transcendentals=0
    )


def call(kernel, outs, scratch, estimate, scalars, operands, grant, aliases=None, waits=()):
    ahead = len(scalars) + len(operands)
    skip = lambda *refs: kernel(*refs[:ahead], *refs[ahead + len(waits) :])
    return pl.pallas_call(
        skip,
        in_specs=[SMEM] * len(scalars) + [VMEM] * len(operands) + [ANY] * len(waits),
        out_specs=[VMEM] * len(outs),
        out_shape=[jax.ShapeDtypeStruct(shape, kind) for shape, kind in outs],
        scratch_shapes=[pltpu.VMEM(shape, kind) for shape, kind in scratch],
        compiler_params=pltpu.CompilerParams(vmem_limit_bytes=grant << 20),
        cost_estimate=estimate,
        input_output_aliases=aliases or {},
    )(*scalars, *operands, *waits)


def saved_shapes(images, rows):
    return [
        ((3, 2, images, KEYS, 384), BF16),
        ((3, 2, images, ROWS, 2 * KEYS), BF16),
        ((3, rows, 256), BF16),
        ((3, rows, 256), F32),
    ]


def pack_weights(chunks, place, w_qkv, w_out, w_fc1, w_fc2):
    rows = w_fc1.shape[0]
    shapes = (rows, 768), (rows, 768 + 2 * chunks[1]), (rows, 2 * (chunks[0] + chunks[2]))
    return pl.pallas_call(
        functools.partial(pack_kernel, chunks),
        in_specs=[SMEM] + [HBM] * 4,
        out_specs=[VMEM] * 3,
        out_shape=[jax.ShapeDtypeStruct(shape, BF16) for shape in shapes],
        scratch_shapes=[
            pltpu.VMEM(w_qkv.shape, BF16),
            pltpu.VMEM(w_out.shape, BF16),
            pltpu.SemaphoreType.DMA((2 + 2 * len(chunks),)),
        ],
        compiler_params=pltpu.CompilerParams(vmem_limit_bytes=63 << 20),
        cost_estimate=cost(1e7, 1e7),
    )(place, w_qkv, w_out, w_fc1, w_fc2.T)


def prepare_tokens(place, lengths, tokens, prompts, key_mask, grads, gain, shift):
    images, _, width = tokens.shape
    rows = images * ROWS
    return call(
        functools.partial(token_kernel, images),
        [((rows, width), BF16)] * 3 + [((images, 1, KEYS), F32)],
        [((ROWS, width), F32)],
        cost(1e7, 1e7),
        (place, lengths),
        (tokens, prompts, key_mask, grads, gain, shift),
        4,
    )


def attend(loader, images, place, normed, visible, stream, b_out, gain, shift, pieces, waits):
    rows, width = normed.shape
    return call(
        functools.partial(attend_kernel, loader, images),
        saved_shapes(images, rows)
        + [((rows, width), F32), ((rows, width), BF16)]
        + [((3, width, 768), BF16), ((width, 768), BF16)],
        [((width, 1024), BF16)],
        cost(8e9, 1e7),
        (place,),
        (normed, visible, stream, b_out, gain, shift, *pieces),
        GRANTS[0],
        waits=waits,
    )


def mlp(loader, slots, place, normed, grad, bias, sums, pieces, waits):
    rows, width = normed.shape
    hidden = bias.shape[1]
    first = sums is None
    sums = () if first else tuple(sums)
    return call(
        functools.partial(mlp_kernel, loader, hidden // slots, slots, first),
        [((rows, width), F32)] * 2,
        [((width, hidden), BF16)] * 2,
        cost(8.0 * rows * width * hidden, 1.6e7),
        (place,),
        (normed, grad, bias, *sums, *pieces),
        GRANTS[2],
        {} if first else {4: 0, 5: 1},
        waits,
    )


def attend_back(
    images, give_kind, place, mid, grad_normed, grad, stream, saved, gain_two, gain_one, weights
):
    rows, width = mid.shape
    return call(
        functools.partial(back_kernel, images),
        [
            ((PROMPTS, width // 2), F32),
            ((PROMPTS, width // 2), give_kind),
            ((images, IMG_TOK - LATE, width), F32),
            ((rows, width), F32),
            ((rows, 3 * 768), BF16),
        ],
        [((rows, width), BF16), ((3, rows, 256), F32)],
        cost(9e9, 2.4e7),
        (place,),
        (mid, grad_normed, grad, stream, *saved, gain_two, gain_one, *weights),
        GRANTS[3],
    )


def finish_rows(images, place, lengths, mid, mlp_out, stream, b_fc2, gain_one, weights, passed):
    width = mid.shape[1]
    return call(
        functools.partial(last_kernel, images),
        [((SEQ, images * width), BF16), ((IMG_TOK, images * width), BF16)],
        [],
        cost(2e9, 1e7),
        (place, lengths),
        (mid, mlp_out, stream, b_fc2, gain_one, weights[0], *passed),
        7,
    )


def add_kernel(*refs):
    *parts, out = refs
    parts = [part[...].astype(F32) for part in parts]
    while len(parts) > 1:
        parts = [parts[at] + parts[at + 1] for at in range(0, len(parts), 2)]
    out[...] = parts[0].astype(BF16)


def add(*parts, waits=()):
    outs = [(parts[-1].shape, BF16)]
    return call(add_kernel, outs, [], cost(0, 0), (), parts, 1, waits=waits)[0]


def sum_prompts(exchange, keep, give, results):
    mine = add(keep, exchange.core(give))
    others = [exchange.swap(mine, dx=dx, dy=dy) for dx, dy in ((1, 0), (0, 1), (1, 1))]
    mine = add(mine, *others, waits=results)
    for dz in (1, 2):
        mine = add(mine, exchange.swap(mine, dz=dz))
    other = exchange.core(mine).astype(F32)
    mine = lax.reduce_precision(mine.astype(F32), 8, 7)
    return jnp.where(
        lax.axis_index("head") % 2 == 0,
        jnp.concatenate([mine, other], axis=1),
        jnp.concatenate([other, mine], axis=1),
    )


def per_device(
    exchange,
    layer_input,
    prompts,
    lengths,
    key_mask,
    ln1_gain,
    ln1_shift,
    w_qkv,
    w_out,
    b_out,
    ln2_gain,
    ln2_shift,
    w_fc1,
    b_fc1,
    w_fc2,
    b_fc2,
    grad_output,
):
    images, _, width = layer_input.shape
    chunks = CHUNKS
    head = lax.axis_index("head")
    core = head % 2

    if exchange is not None:
        depth = exchange.depth
        dp = lax.axis_index("dp")
        place = [dp // 2, dp % 2, head // 2, core]
    else:
        depth = 0
        place = [0, 0, 0, core]
    place = jnp.stack([jnp.asarray(value, jnp.int32) for value in (*place, head * images)])

    own, both, later = pack_weights(chunks, place, w_qkv, w_out, w_fc1, w_fc2)
    if exchange is not None:
        gather = Gather(exchange, own, both, later, b_fc1)
    else:

        def gather_whole(piece):
            rows = lax.all_gather(piece, "dp", axis=0, tiled=True)
            held = Held(None)
            held.arrays = [lax.all_gather(rows, "head", axis=0)]
            held.plan = [(0, ALL, [(dy, c) for dy in (0, 1) for c in (0, 1)])]
            return held

        attn = gather_whole(own)
        split = 2 * chunks[0]
        gathered = [gather_whole(piece) for piece in (later[:, :split], both[:, 768:], later[:, split:])]
        bias = lax.all_gather(b_fc1, "head", axis=0)

    row = lambda vector: vector.reshape(1, -1)
    stream, normed, grad, visible = prepare_tokens(
        place, lengths, layer_input, prompts, key_mask, grad_output, row(ln1_gain), row(ln1_shift)
    )
    waits = ()
    if exchange is not None:
        attn, (normed, visible, stream, grad) = gather.attention(normed, visible, stream, grad)
        bias = gather.bias
        waits = (bias,)
    load_attn = Loader(attn.plan, depth)
    *saved, mid, normed_mlp, wide, out = attend(
        load_attn, images, place, normed, visible, stream,
        row(b_out), row(ln2_gain), row(ln2_shift), attn.arrays, waits,
    )
    if exchange is None:
        order = [(bias, gathered[index], 4, index) for index in range(3)]
    else:
        normed_mlp = gather.round_seven(normed_mlp)
        even, odd = bias[0::2], bias[1::2]
        biases = jnp.where(core == 0, even, odd), jnp.where(core == 0, odd, even)
        both = Held(None)
        both.arrays = gather.halves[0].arrays + gather.halves[1].arrays
        both.plan = gather.halves[0].plan + gather.halves[1].plan
        order = [(bias, both, 4, 0)]
        order += [(bias, gather.parts[index], 4, index) for index in (1, 2)]
    sums = None
    for values, held, slots, index in order:
        if exchange is not None and index == 1:
            sums[0] = gather.round_eight(sums[0])
        chunk_bias = row(values[:, sum(chunks[:index]) : sum(chunks[: index + 1])])
        loader = Loader(held.plan, depth)
        sums = mlp(loader, slots, place, normed_mlp, grad, chunk_bias, sums, held.arrays, ())
        sums = list(sums)
    weights = (wide, out)
    keep, give, *passed = attend_back(
        images, BF16 if exchange is not None else F32, place, mid, sums[1], grad, stream, saved,
        row(ln2_gain), row(ln1_gain), weights,
    )
    results = finish_rows(
        images, place, lengths, mid, sums[0], stream, row(b_fc2), row(ln1_gain), weights, passed
    )
    if exchange is not None:
        total = sum_prompts(exchange, keep, give, results)
    else:
        total = lax.psum(jnp.concatenate([keep, give], axis=1), BOTH)
    results = [result.reshape(result.shape[0], images, width) for result in results]
    return (*(jnp.transpose(result, (1, 0, 2)) for result in results), total)


def solution(mesh):
    dp, head = mesh.shape["dp"], mesh.shape["head"]
    exchange = Exchange(dp, head) if (dp, head) == (8, 4) else None
    placed = (
        P(BOTH, None, None),
        P(),
        P("dp"),
        P("dp", None),
        P(),
        P(),
        P(None, "dp", "head"),
        P("head", "dp"),
        P(),
        P(),
        P(),
        P("dp", "head"),
        P("head"),
        P("head", "dp"),
        P(),
        P(BOTH, None, None),
    )
    return jax.shard_map(
        functools.partial(per_device, exchange),
        mesh=mesh,
        in_specs=placed,
        out_specs=(P(BOTH, None, None), P(BOTH, None, None), P()),
        check_vma=False,
    )
```
